256 devices in a mesh: row: 16 (over x, y_lo, core), col: 16 (over y_hi, z).
Axes of the slice: x: 4, y: 4 (y_hi: 2, y_lo: 2; y = y_hi * 2 + y_lo), z: 8, core: 2. Of those that a mesh axis runs over, the one named last changes fastest.
Arguments:
- blocks: bfloat16 [16, 16, 256, 128, 128], P('row', 'col'), may hold values from -0.0234375 to 0.0234375
- block_rows: int32 [16, 16, 256], P('row', 'col'), may hold values from 0 to 31, as said below
- block_cols: int32 [16, 16, 256], P('row', 'col'), may hold values from 0 to 31, as said below
- block_count: int32 [16, 16], P('row', 'col'), may hold values from 64 to 256, as said below
- probes: float32 [64, 65536], P(None, ('row', 'col')), may hold values from -6 to 6
- t_prev: float32 [64, 65536], P(None, ('row', 'col')), may hold values from -6 to 6
- t_cur: float32 [64, 65536], P(None, ('row', 'col')), may hold values from -6 to 6
- accum: float32 [64, 65536], P(None, ('row', 'col')), may hold values from -6 to 6
- coeffs: float32 [2], replicated, may hold values from 0.5 to 1.5
Outputs:
- t_next: float32 [64, 65536], P(None, ('row', 'col'))
- t_after: float32 [64, 65536], P(None, ('row', 'col'))
- accum_out: float32 [64, 65536], P(None, ('row', 'col'))
- moments: float32 [2, 64], replicated
The draws below stay inside these ranges and needn't reach their ends.
Inputs may be any that keep to these rules, and one draw needn't show every extreme that they name: `block_rows`: within one device the live slots name distinct blocks; block rows lie in [0, 32) and block columns in [0, 32). `block_cols`: pairs with block_rows: within one device the live slots name distinct blocks. `block_count`: some device has all 256 slots live in every draw.
All inputs are finite; a program needn't handle non-finite values.
Results may differ from the reference program's by a relative error of at most 0.0025.
Values may be sent and summed in bfloat16 or wider, within the bound.
A program may use at most 64 MiB of HBM per device.

```python
import jax
import jax.numpy as jnp
from jax import lax

BS = 128
PROBES = 64
PB = 2
SLOTS_ROW = 8
LROWS = 32
LCOLS = 32
MAXB = 256
ORDER = 65536
N_ROW = 16
N_COL = 16


def pattern_places(key):
    grid_rows = LCOLS // PB
    grid_cols = LROWS // PB
    sub_keys = jax.random.split(jax.random.fold_in(key, 17), grid_rows * grid_cols)

    def device_slots(sub_key):
        return jax.random.permutation(sub_key, LROWS * LCOLS)[:MAXB]
    places = jax.vmap(device_slots)(sub_keys)
    return places.reshape(grid_rows, grid_cols, MAXB).astype(jnp.int32)


def draw_block_rows(key, part):
    return (pattern_places(key) // LCOLS).astype(jnp.int32)


def draw_block_cols(key, part):
    return (pattern_places(key) % LCOLS).astype(jnp.int32)


def draw_block_count(key, part):
    grid_rows = LCOLS // PB
    grid_cols = LROWS // PB
    devices_all = grid_rows * grid_cols
    drawn = jax.random.randint(jax.random.fold_in(key, 29), (devices_all,), MAXB // 4, MAXB + 1)
    fullest = jax.random.randint(jax.random.fold_in(key, 31), (), 0, devices_all)
    drawn = jnp.where(jnp.arange(devices_all) == fullest, MAXB, drawn)
    return drawn.reshape(grid_rows, grid_cols).astype(jnp.int32)


def block_levels(key, extent, shards, least, largest):
    loudness, own = 1.0, jax.random.fold_in(key, 6)
    for position, blocks in shards:
        draws = jnp.exp(jax.random.uniform(jax.random.fold_in(own, position), (blocks,), jnp.float32, least / len(shards), largest / len(shards)))
        loudness = loudness * jnp.repeat(draws, extent[position] // blocks).reshape([-1 if axis == position else 1 for axis in range(len(extent))])
    return loudness


def bell_draw(key, shape, spread, limit, pieces=(), held_as=jnp.bfloat16):
    entries = jax.random.normal(key, shape, jnp.float32) * spread
    if len(pieces) > 0:
        entries = block_levels(key, shape, pieces, -0.22, 0.18) * entries
    return jnp.clip(entries, min=-limit, max=limit).astype(held_as)


def setup_inputs(seed: int = 0) -> dict:
    key_list = jax.random.split(jax.random.key(seed), 10)
    return {
        "blocks": bell_draw(key_list[0], (N_ROW, N_COL, MAXB, BS, BS), (4 * BS * N_COL * SLOTS_ROW) ** -0.5, 0.0234375, ((0, 16), (1, 16))),
        "block_rows": draw_block_rows(jax.random.fold_in(key_list[9], 71), 0),
        "block_cols": draw_block_cols(jax.random.fold_in(key_list[9], 71), 0),
        "block_count": draw_block_count(jax.random.fold_in(key_list[9], 71), 0),
        "probes": bell_draw(key_list[4], (PROBES, ORDER), 1.0, 6.0, ((1, 256),), jnp.float32),
        "t_prev": bell_draw(key_list[5], (PROBES, ORDER), 1.0, 6.0, ((1, 256),), jnp.float32),
        "t_cur": bell_draw(key_list[6], (PROBES, ORDER), 1.0, 6.0, ((1, 256),), jnp.float32),
        "accum": bell_draw(key_list[7], (PROBES, ORDER), 1.0, 6.0, ((1, 256),), jnp.float32),
        "coeffs": jnp.clip(jax.random.uniform(key_list[8], (2,), jnp.float32, 0.5, 1.5), 0.5, 1.5),
    }


def product(blocks, block_rows, block_cols, block_count, vectors):
    split_vec = vectors.astype(jnp.bfloat16).reshape(PROBES, N_ROW, N_COL, PB * BS)
    slot_ids = jnp.arange(MAXB, dtype=jnp.int32)

    def per_row(row_idx):
        def per_col(total, col_idx):
            column_set = lax.dynamic_index_in_dim(split_vec, col_idx, 2, keepdims=False)
            column_set = column_set.reshape(PROBES, LCOLS, BS)
            tiles = blocks[row_idx, col_idx].astype(jnp.float32)
            row_ids = block_rows[row_idx, col_idx]
            col_ids = block_cols[row_idx, col_idx]
            alive = (slot_ids < block_count[row_idx, col_idx]).astype(jnp.float32)
            picked = jnp.take(column_set, col_ids, axis=1).astype(jnp.float32)
            contrib = jnp.einsum("pgj,gij->pgi", picked, tiles) * alive[None, :, None]
            partial_value = jnp.zeros((PROBES, LROWS, BS), jnp.float32).at[:, row_ids, :].add(contrib)
            return total + partial_value, None

        start = jnp.zeros((PROBES, LROWS, BS), jnp.float32)
        total, _ = lax.scan(per_col, start, jnp.arange(N_COL, dtype=jnp.int32))
        return total.reshape(PROBES, LROWS * BS)

    row_sets = lax.map(per_row, jnp.arange(N_ROW, dtype=jnp.int32))
    return jnp.transpose(row_sets, (1, 0, 2)).reshape(PROBES, ORDER)


def reference(blocks, block_rows, block_cols, block_count, probes, t_prev, t_cur, accum, coeffs):
    t_next = 2.0 * product(blocks, block_rows, block_cols, block_count, t_cur) - t_prev
    t_after = 2.0 * product(blocks, block_rows, block_cols, block_count, t_next) - t_cur
    accum_out = accum + coeffs[0] * t_next + coeffs[1] * t_after
    scale = float(ORDER) ** -0.5
    first = jnp.sum(probes * t_next, axis=1) * scale
    second = jnp.sum(probes * t_after, axis=1) * scale
    moments = jnp.stack([first, second])
    return t_next, t_after, accum_out, moments
```

```python
import jax
import jax.numpy as jnp
from jax import lax
from jax.experimental import pallas as pl
from jax.experimental.pallas import tpu as pltpu
from jax.sharding import PartitionSpec as P

MESH = pl.DeviceIdType.MESH
F32 = jnp.float32
BF16 = jnp.bfloat16
BS = 128
PROBES = 64
MAXB = 256
LROWS = 32
PAIRS = 144
TAB = 384
UNROLL = 24
ROW_OFFS = ((2, 1), (2, 0), (1, 1), (3, 1), (1, 0), (3, 0), (0, 1))
COL_OFFS = (
    (1, 4), (0, 4), (1, 3), (1, 5), (0, 3), (0, 5), (1, 2), (1, 6),
    (0, 2), (0, 6), (1, 1), (1, 7), (0, 1), (0, 7), (1, 0),
)


def iota(shape, axis):
    return lax.broadcasted_iota(jnp.int32, shape, axis)


def to_sub(row):
    n = row.shape[1]
    eye = iota((n, n), 0) == iota((n, n), 1)
    return jnp.sum(jnp.where(eye, row, 0), axis=1, keepdims=True)


def tables(rows, cols, count):
    total = lambda mask, value, axis: jnp.sum(jnp.where(mask, value, 0), axis=axis, keepdims=True)
    live = iota((1, MAXB), 1) < count
    row_l = jnp.where(live, rows, 1000)
    row_c, col_c = to_sub(row_l), to_sub(cols)
    rho = total((row_c == row_l) & (col_c < cols), 1, 0)
    hit = iota((LROWS, MAXB), 0) == row_l
    pairs_c = (total(hit, 1, 1) + 1) >> 1
    i0, i1 = iota((LROWS, BS), 0), iota((LROWS, BS), 1)
    base_l = total(i0 < i1, pairs_c, 0)
    pairs_l = total(i0 == i1, pairs_c, 0)
    base_c = total(i0 == i1, base_l, 1)
    pos = jnp.where(live, 2 * total(hit, base_c, 0) + rho, -1)
    at = to_sub(pos) == iota((MAXB, TAB), 1)
    slot_l = MAXB + total(at, iota((MAXB, TAB), 0) - MAXB, 0)
    col_l = total(at, col_c, 0)
    first = (base_c == iota((LROWS, TAB), 1)) & (pairs_c > 0)
    keep_l = 1 - total(first, 1, 0)
    last_l = jnp.where(pairs_l > 0, base_l + pairs_l - 1, PAIRS)
    return slot_l, col_l, keep_l, last_l


def kernel(
    blocks, rows, cols, count, probes, t_prev, t_cur, accum, coeffs,
    o_next, o_after, o_accum, o_mom,
    mat, vec0, vec1, part, out_buf, in_buf, mom_row, mom_col, mom_own,
    itab, ftab, itab_s, ftab_s,
    mat_sem, tab_sem, ag_s, ag_r, fw_s, fw_r, rs_s, rs_r, ma_s, ma_r, mb_s, mb_r,
):
    r, q = lax.axis_index("row"), lax.axis_index("col")
    x, yl, core = r // 4, (r // 2) % 2, r % 2
    yh, z = q // 8, q % 8

    def row_id(dx, dy, dc=0):
        return ((x + dx) % 4) * 4 + ((yl + dy) % 2) * 2 + (core + dc) % 2

    def col_id(dy, dz):
        return ((yh + dy) % 2) * 8 + (z + dz) % 8

    vec = (vec0, vec1)
    barrier = pltpu.get_barrier_semaphore()
    for i in range(1, 16):
        pl.semaphore_signal(barrier, inc=1, device_id=((r + i) % 16, q), device_id_type=MESH)
        pl.semaphore_signal(barrier, inc=1, device_id=(r, (q + i) % 16), device_id_type=MESH)

    load = pltpu.make_async_copy(blocks, mat.at[pl.ds(0, MAXB)], mat_sem)
    load.start()

    def put_own(step, value):
        own = value.astype(BF16)
        vec[step][2 * r] = own[:, :BS]
        vec[step][2 * r + 1] = own[:, BS:]

    put_own(0, t_cur[...])
    mat[MAXB] = jnp.zeros((BS, BS), BF16)
    part[PAIRS] = jnp.zeros((PROBES, BS), F32)
    slot_l, col_l, keep_l, last_l = tables(rows[...], cols[...], count[0])
    itab[0:1, :] = slot_l
    itab[1:2, :] = col_l
    itab[2:3, 0:BS] = last_l
    ftab[0:1, :] = keep_l.astype(F32)

    pl.semaphore_wait(barrier, 30)

    def remote(src, dst, s_sem, r_sem, dev):
        copy = pltpu.make_async_remote_copy(
            src_ref=src, dst_ref=dst, send_sem=s_sem, recv_sem=r_sem,
            device_id=dev, device_id_type=MESH,
        )
        copy.start()
        return copy

    def gather(step):
        sent = []
        own = vec[step].at[pl.ds(2 * r, 2)]
        mate = (row_id(0, 0, 1), q)
        for n, (dx, dy) in enumerate(ROW_OFFS):
            sent.append(remote(own, own, ag_s.at[step, n], ag_r.at[step, n], (row_id(dx, dy), q)))
        last = len(ROW_OFFS)
        passed = [remote(own, own, fw_s.at[step, last], fw_r.at[step, last], mate)]
        for n in reversed(range(last)):
            dx, dy = ROW_OFFS[n]
            sent[n].wait_recv()
            got = vec[step].at[pl.ds(2 * row_id(4 - dx, dy), 2)]
            passed.append(remote(got, got, fw_s.at[step, n], fw_r.at[step, n], mate))
        for copy in passed:
            copy.wait_recv()
        return sent, passed

    def multiply(step):
        def body(i, acc):
            for u in range(UNROLL):
                n = i * UNROLL + u
                a, b = itab_s[0, 2 * n], itab_s[0, 2 * n + 1]
                c, d = itab_s[1, 2 * n], itab_s[1, 2 * n + 1]
                lhs = jnp.concatenate([vec[step][c], vec[step][d]], axis=1)
                rhs = jnp.concatenate([mat[a], mat[b]], axis=1)
                prod = lax.dot_general(
                    lhs, rhs, (((1,), (1,)), ((), ())), preferred_element_type=F32
                )
                acc = acc * ftab_s[0, n] + prod
                part[n] = acc
            return acc

        lax.fori_loop(0, PAIRS // UNROLL, body, jnp.zeros((PROBES, BS), F32))

    def piece(c):
        lo = part[itab_s[2, 2 * c]]
        hi = part[itab_s[2, 2 * c + 1]]
        return jnp.concatenate([lo, hi], axis=1)

    def scatter(step):
        sent = []
        for n, (dy, dz) in enumerate(COL_OFFS):
            c = col_id(dy, dz)
            out_buf[step, n] = piece(c).astype(BF16)
            sent.append(
                remote(out_buf.at[step, n], in_buf.at[step, n], rs_s.at[step, n], rs_r.at[step, n], (r, c))
            )
        total = piece(q)
        for n in reversed(range(len(COL_OFFS))):
            sent[n].wait_recv()
            total = total + in_buf[step, n].astype(F32)
        return total, sent

    sent0, passed0 = gather(0)
    tab_i = pltpu.make_async_copy(itab, itab_s, tab_sem.at[0])
    tab_f = pltpu.make_async_copy(ftab, ftab_s, tab_sem.at[1])
    tab_i.start()
    tab_f.start()
    tab_i.wait()
    tab_f.wait()
    load.wait()
    multiply(0)
    total, out0 = scatter(0)
    t_next = 2.0 * total - t_prev[...]
    put_own(1, t_next)
    sent1, passed1 = gather(1)
    o_next[...] = t_next
    first = jnp.sum(probes[...] * t_next, axis=1, keepdims=True)
    multiply(1)
    total, out1 = scatter(1)
    t_after = 2.0 * total - t_cur[...]
    o_after[...] = t_after
    o_accum[...] = accum[...] + coeffs[0] * o_next[...] + coeffs[1] * t_after
    second = jnp.sum(probes[...] * t_after, axis=1, keepdims=True)

    diag = iota((PROBES, BS), 0) == iota((PROBES, BS), 1)
    flat = lambda m: jnp.sum(jnp.where(diag, m, 0.0), axis=0, keepdims=True)
    mom_own[0, 0:1, :] = flat(first)
    mom_own[0, 1:2, :] = flat(second)
    copies = []
    for i in range(1, 16):
        dev = ((r + i) % 16, q)
        copies.append(remote(mom_own.at[0], mom_row.at[r], ma_s.at[i], ma_r.at[i], dev))
    mom_row[r] = mom_own[0]
    for copy in copies:
        copy.wait_recv()
    mom_own[1] = jnp.sum(mom_row[...], axis=0)
    more = []
    for i in range(1, 16):
        dev = (r, (q + i) % 16)
        more.append(remote(mom_own.at[1], mom_col.at[q], mb_s.at[i], mb_r.at[i], dev))
    mom_col[q] = mom_own[1]
    for copy in more:
        copy.wait_recv()
    scale = float(LROWS * BS * 16) ** -0.5
    o_mom[...] = jnp.sum(mom_col[...], axis=0)[0:2, 0:PROBES] * scale
    for copy in copies + more + sent0 + passed0 + sent1 + passed1 + out0 + out1:
        copy.wait_send()


def local(blocks, block_rows, block_cols, block_count, probes, t_prev, t_cur, accum, coeffs):
    vmem = pl.BlockSpec(memory_space=pltpu.VMEM)
    smem = pl.BlockSpec(memory_space=pltpu.SMEM)
    width = t_cur.shape[1]
    big = jax.ShapeDtypeStruct((PROBES, width), F32)
    sem = pltpu.SemaphoreType.DMA
    return pl.pallas_call(
        kernel,
        out_shape=(big, big, big, jax.ShapeDtypeStruct((2, PROBES), F32)),
        in_specs=[pl.BlockSpec(memory_space=pl.ANY), vmem, vmem, smem, vmem, vmem, vmem, vmem, smem],
        out_specs=(vmem, vmem, vmem, vmem),
        scratch_shapes=[
            pltpu.VMEM((MAXB + 1, BS, BS), BF16),
            pltpu.VMEM((LROWS, PROBES, BS), BF16),
            pltpu.VMEM((LROWS, PROBES, BS), BF16),
            pltpu.VMEM((PAIRS + 1, PROBES, BS), F32),
            pltpu.VMEM((2, 15, PROBES, width), BF16),
            pltpu.VMEM((2, 15, PROBES, width), BF16),
            pltpu.VMEM((16, 8, BS), F32),
            pltpu.VMEM((16, 8, BS), F32),
            pltpu.VMEM((2, 8, BS), F32),
            pltpu.VMEM((8, TAB), jnp.int32),
            pltpu.VMEM((8, TAB), F32),
            pltpu.SMEM((8, TAB), jnp.int32),
            pltpu.SMEM((8, TAB), F32),
            sem,
            sem((2,)),
            sem((2, 7)), sem((2, 7)), sem((2, 8)), sem((2, 8)),
            sem((2, 15)), sem((2, 15)),
            sem((16,)), sem((16,)), sem((16,)), sem((16,)),
        ],
        compiler_params=pltpu.CompilerParams(
            collective_id=0, has_side_effects=True, vmem_limit_bytes=48 << 20
        ),
    )(
        blocks.reshape(MAXB, BS, BS), block_rows.reshape(1, MAXB), block_cols.reshape(1, MAXB),
        block_count.reshape(1), probes, t_prev, t_cur, accum, coeffs,
    )


def solution(mesh):
    split = P(None, ("row", "col"))
    return jax.shard_map(
        local,
        mesh=mesh,
        in_specs=(
            P("row", "col", None, None, None), P("row", "col", None), P("row", "col", None),
            P("row", "col"), split, split, split, split, P(),
        ),
        out_specs=(split, split, split, P()),
        check_vma=False,
    )
```

```python
import jax
import jax.numpy as jnp
from jax import lax
from jax.experimental import pallas as pl
from jax.experimental.pallas import tpu as pltpu
from jax.sharding import PartitionSpec as P

MESH = pl.DeviceIdType.MESH
F32 = jnp.float32
BF16 = jnp.bfloat16
BS = 128
PROBES = 64
MAXB = 256
LROWS = 32
PAIRS = 144
TAB = 384
UNROLL = 24
ROW_OFFS = ((2, 1), (2, 0), (1, 1), (3, 1), (1, 0), (3, 0), (0, 1))
COL_OFFS = (
    (1, 4), (0, 4), (1, 3), (1, 5), (0, 3), (0, 5), (1, 2), (1, 6),
    (0, 2), (0, 6), (1, 1), (1, 7), (0, 1), (0, 7), (1, 0),
)
PACK = 8


def iota(shape, axis):
    return lax.broadcasted_iota(jnp.int32, shape, axis)


def to_sub(row):
    n = row.shape[1]
    eye = iota((n, n), 0) == iota((n, n), 1)
    return jnp.sum(jnp.where(eye, row, 0), axis=1, keepdims=True)


def tables(rows, cols, count):
    total = lambda mask, value, axis: jnp.sum(jnp.where(mask, value, 0), axis=axis, keepdims=True)
    live = iota((1, MAXB), 1) < count
    row_l = jnp.where(live, rows, 1000)
    row_c, col_c = to_sub(row_l), to_sub(cols)
    rho = total((row_c == row_l) & (col_c < cols), 1, 0)
    hit = iota((LROWS, MAXB), 0) == row_l
    pairs_c = (total(hit, 1, 1) + 1) >> 1
    i0, i1 = iota((LROWS, BS), 0), iota((LROWS, BS), 1)
    base_l = total(i0 < i1, pairs_c, 0)
    pairs_l = total(i0 == i1, pairs_c, 0)
    base_c = total(i0 == i1, base_l, 1)
    pos = jnp.where(live, 2 * total(hit, base_c, 0) + rho, -1)
    at = to_sub(pos) == iota((MAXB, TAB), 1)
    slot_l = MAXB + total(at, iota((MAXB, TAB), 0) - MAXB, 0)
    col_l = total(at, col_c, 0)
    first = (base_c == iota((LROWS, TAB), 1)) & (pairs_c > 0)
    keep_l = 1 - total(first, 1, 0)
    last_l = jnp.where(pairs_l > 0, base_l + pairs_l - 1, PAIRS)
    return slot_l, col_l, keep_l, last_l


def kernel(
    blocks, rows_h, cols_h, count_h, probes_h, t_prev_h, t_cur_h,
    o_first, o_second, o_mom,
    mat, packed, vec0, vec1, part, out_buf, in_buf, probes_all, mom_col, mom_row, mom_own,
    rows, cols, count, probes, t_prev, t_cur,
    itab, ftab, itab_s, ftab_s,
    in_sem, tab_sem, ag_s, ag_r, fw_s, fw_r, rs_s, rs_r, pr_s, pr_r, ma_s, ma_r, mb_s, mb_r,
    near_sem, mid_sem, far_sem,
):
    r, q = lax.axis_index("row"), lax.axis_index("col")
    x, yl, core = r // 4, (r // 2) % 2, r % 2
    yh, z = q // 8, q % 8
    vec = (vec0, vec1)

    def row_id(dx, dy, dc=0):
        return ((x + dx) % 4) * 4 + ((yl + dy) % 2) * 2 + (core + dc) % 2

    def col_id(dy, dz):
        return ((yh + dy) % 2) * 8 + (z + dz) % 8

    def signal(sem, dev):
        pl.semaphore_signal(sem, inc=1, device_id=dev, device_id_type=MESH)

    def remote(src, dst, s_sem, r_sem, dev):
        copy = pltpu.make_async_remote_copy(
            src_ref=src, dst_ref=dst, send_sem=s_sem, recv_sem=r_sem,
            device_id=dev, device_id_type=MESH,
        )
        copy.start()
        return copy

    barrier = pltpu.get_barrier_semaphore()
    close = [(r, col_id(0, 1)), (r, col_id(0, 7)), (r, col_id(1, 0))]
    for dev in close + [((r + i) % 16, q) for i in range(1, 16)]:
        signal(barrier, dev)

    loads = []
    for n, (src, dst) in enumerate((
        (t_cur_h, t_cur), (rows_h, rows), (cols_h, cols), (count_h, count),
        (blocks, mat.at[pl.ds(0, MAXB)]), (probes_h, probes), (t_prev_h, t_prev),
    )):
        copy = pltpu.make_async_copy(src, dst, in_sem.at[n])
        copy.start()
        loads.append(copy)

    def put_own(step, value):
        own = value.astype(BF16)
        vec[step][2 * r] = own[:, :BS]
        vec[step][2 * r + 1] = own[:, BS:]

    def gather_start(step):
        own = vec[step].at[pl.ds(2 * r, 2)]
        mate = (row_id(0, 0, 1), q)
        sent = []
        for n, (dx, dy) in enumerate(ROW_OFFS):
            sent.append(remote(own, own, ag_s.at[step, n], ag_r.at[step, n], (row_id(dx, dy), q)))
        last = len(ROW_OFFS)
        passed = [remote(own, own, fw_s.at[step, last], fw_r.at[step, last], mate)]
        return sent, passed

    def pass_on(step, sent, passed, which):
        mate = (row_id(0, 0, 1), q)
        for n in which:
            dx, dy = ROW_OFFS[n]
            sent[n].wait_recv()
            got = vec[step].at[pl.ds(2 * row_id(4 - dx, dy), 2)]
            passed.append(remote(got, got, fw_s.at[step, n], fw_r.at[step, n], mate))

    def share_probes(offs):
        sent = []
        for dy, dz in offs:
            n = dy * 8 + dz
            sent.append(remote(probes_all.at[q], probes_all.at[q], pr_s.at[n], pr_r.at[n], (r, col_id(dy, dz))))
        return sent

    def pack(lo, hi):
        def body(i, _):
            for u in range(PACK):
                n = i * PACK + u
                packed[n] = mat[itab_s[0, n]].T
            return 0

        lax.fori_loop(lo // PACK, hi // PACK, body, 0)

    def multiply(step):
        def body(i, acc):
            for u in range(UNROLL):
                n = i * UNROLL + u
                c, d = itab_s[1, 2 * n], itab_s[1, 2 * n + 1]
                lhs = jnp.concatenate([vec[step][c], vec[step][d]], axis=1)
                rhs = packed[pl.ds(2 * n, 2)].reshape(2 * BS, BS)
                acc = acc * ftab_s[0, n] + jnp.dot(lhs, rhs, preferred_element_type=F32)
                part[n] = acc
            return acc

        lax.fori_loop(0, PAIRS // UNROLL, body, jnp.zeros((PROBES, BS), F32))

    def piece(c):
        lo = part[itab_s[2, 2 * c]]
        hi = part[itab_s[2, 2 * c + 1]]
        return jnp.concatenate([lo, hi], axis=1)

    def scatter_start(step, offs):
        sent = []
        for dy, dz in offs:
            n, c = COL_OFFS.index((dy, dz)), col_id(dy, dz)
            out_buf[step, n] = piece(c).astype(BF16)
            sent.append(
                remote(out_buf.at[step, n], in_buf.at[step, n], rs_s.at[step, n], rs_r.at[step, n], (r, c))
            )
        return sent

    def scatter_sum(step, sent):
        total = piece(q)
        for n in reversed(range(len(COL_OFFS))):
            sent[n].wait_recv()
            total = total + in_buf[step, n].astype(F32)
        return total

    loads[0].wait()
    put_own(0, t_cur[...])
    pl.semaphore_wait(barrier, 18)
    sent0, passed0 = gather_start(0)
    for dev in close:
        signal(near_sem, dev)

    mat[MAXB] = jnp.zeros((BS, BS), BF16)
    part[PAIRS] = jnp.zeros((PROBES, BS), F32)
    for copy in loads[1:4]:
        copy.wait()
    slot_l, col_l, keep_l, last_l = tables(rows[...], cols[...], count[...])
    itab[0:1, :] = slot_l
    itab[1:2, :] = col_l
    itab[2:3, 0:BS] = last_l
    ftab[0:1, :] = keep_l.astype(F32)
    for copy in loads[4:]:
        copy.wait()
    probes_all[q] = probes[...].astype(BF16)
    pl.semaphore_wait(near_sem, 3)
    for dz in (2, 6):
        signal(mid_sem, (r, col_id(0, dz)))
    tab_i = pltpu.make_async_copy(itab, itab_s, tab_sem.at[0])
    tab_f = pltpu.make_async_copy(ftab, ftab_s, tab_sem.at[1])
    tab_i.start()
    tab_f.start()
    tab_i.wait()
    tab_f.wait()
    pack(0, 96)
    pass_on(0, sent0, passed0, (6, 5, 4))
    pl.semaphore_wait(mid_sem, 2)
    signal(far_sem, (r, col_id(1, 0)))
    shared = share_probes([(0, dz) for dz in (4, 3, 5, 2, 6, 1, 7)])
    pack(96, 192)
    pass_on(0, sent0, passed0, (3, 2))
    pack(192, 288)
    pass_on(0, sent0, passed0, (1, 0))
    for copy in passed0:
        copy.wait_recv()
    multiply(0)
    pl.semaphore_wait(far_sem, 1)
    out0 = scatter_start(0, COL_OFFS)
    total = scatter_sum(0, out0)
    t_next = 2.0 * total - t_prev[...]
    put_own(1, t_next)
    sent1, passed1 = gather_start(1)
    shared += share_probes([(1, dz) for dz in (4, 3, 5, 2, 6, 1, 7, 0)])
    o_first[...] = total
    first = jnp.sum(probes[...] * t_next, axis=1, keepdims=True)
    before = jnp.sum(probes[...] * t_cur[...], axis=1, keepdims=True)
    pass_on(1, sent1, passed1, (6, 5, 4, 3, 2, 1, 0))
    for copy in passed1:
        copy.wait_recv()
    multiply(1)
    out1 = scatter_start(1, COL_OFFS[:4])

    for copy in shared:
        copy.wait_recv()

    def weigh(c, acc):
        return acc + probes_all[c].astype(F32) * piece(c)

    held = lax.fori_loop(0, 16, weigh, jnp.zeros((PROBES, 2 * BS), F32))
    second = 2.0 * jnp.sum(held, axis=1, keepdims=True) - before
    i0, i1 = iota((PROBES, BS), 0), iota((PROBES, BS), 1)
    both = jnp.where(i0 == i1, first, 0.0) + jnp.where(i0 + PROBES == i1, second, 0.0)
    mine = jnp.sum(both, axis=0, keepdims=True)
    mom_own[0] = mine
    mom_col[q] = mine
    copies = []
    for n, (dy, dz) in enumerate(COL_OFFS):
        dev = (r, col_id(dy, dz))
        copies.append(remote(mom_own.at[0], mom_col.at[q], ma_s.at[n], ma_r.at[n], dev))
    out1 += scatter_start(1, COL_OFFS[4:])
    for copy in copies:
        copy.wait_recv()
    mine = jnp.sum(mom_col[...], axis=0)
    mom_own[1] = mine
    mom_row[r] = mine
    more = []
    for i in range(1, 16):
        dev = ((r + i) % 16, q)
        more.append(remote(mom_own.at[1], mom_row.at[r], mb_s.at[i], mb_r.at[i], dev))
    o_second[...] = scatter_sum(1, out1)
    for copy in more:
        copy.wait_recv()
    scale = float(LROWS * BS * 16) ** -0.5
    summed = jnp.sum(mom_row[...], axis=0) * scale
    o_mom[0:1, :] = summed[:, :PROBES]
    o_mom[1:2, :] = summed[:, PROBES:]
    for copy in copies + more + shared + sent0 + passed0 + sent1 + passed1 + out0 + out1:
        copy.wait_send()


def local(blocks, block_rows, block_cols, block_count, probes, t_prev, t_cur, accum, coeffs):
    vmem = pl.BlockSpec(memory_space=pltpu.VMEM)
    hbm = pl.BlockSpec(memory_space=pltpu.HBM)
    width = t_cur.shape[1]
    big = jax.ShapeDtypeStruct((PROBES, width), F32)
    sem = pltpu.SemaphoreType.DMA
    regular = pltpu.SemaphoreType.REGULAR
    first, second, moments = pl.pallas_call(
        kernel,
        out_shape=(big, big, jax.ShapeDtypeStruct((2, PROBES), F32)),
        in_specs=[hbm] * 7,
        out_specs=(vmem, vmem, vmem),
        scratch_shapes=[
            pltpu.VMEM((MAXB + 1, BS, BS), BF16),
            pltpu.VMEM((2 * PAIRS, BS, BS), BF16),
            pltpu.VMEM((LROWS, PROBES, BS), BF16),
            pltpu.VMEM((LROWS, PROBES, BS), BF16),
            pltpu.VMEM((PAIRS + 1, PROBES, BS), F32),
            pltpu.VMEM((2, 15, PROBES, width), BF16),
            pltpu.VMEM((2, 15, PROBES, width), BF16),
            pltpu.VMEM((16, PROBES, width), BF16),
            pltpu.VMEM((16, 1, BS), F32),
            pltpu.VMEM((16, 1, BS), F32),
            pltpu.VMEM((2, 1, BS), F32),
            pltpu.VMEM((1, MAXB), jnp.int32),
            pltpu.VMEM((1, MAXB), jnp.int32),
            pltpu.VMEM((1, 1), jnp.int32),
            pltpu.VMEM((PROBES, width), F32),
            pltpu.VMEM((PROBES, width), F32),
            pltpu.VMEM((PROBES, width), F32),
            pltpu.VMEM((8, TAB), jnp.int32),
            pltpu.VMEM((8, TAB), F32),
            pltpu.SMEM((8, TAB), jnp.int32),
            pltpu.SMEM((8, TAB), F32),
            sem((7,)),
            sem((2,)),
            sem((2, 7)), sem((2, 7)), sem((2, 8)), sem((2, 8)),
            sem((2, 15)), sem((2, 15)), sem((16,)), sem((16,)),
            sem((16,)), sem((16,)), sem((16,)), sem((16,)),
            regular, regular, regular,
        ],
        compiler_params=pltpu.CompilerParams(
            collective_id=0, has_side_effects=True, vmem_limit_bytes=60 << 20
        ),
    )(
        blocks.reshape(MAXB, BS, BS), block_rows.reshape(1, MAXB), block_cols.reshape(1, MAXB),
        block_count, probes, t_prev, t_cur,
    )
    t_next = 2.0 * first - t_prev
    t_after = 2.0 * second - t_cur
    accum_out = accum + coeffs[0] * t_next + coeffs[1] * t_after
    return t_next, t_after, accum_out, moments


def solution(mesh):
    split = P(None, ("row", "col"))
    return jax.shard_map(
        local,
        mesh=mesh,
        in_specs=(
            P("row", "col", None, None, None), P("row", "col", None), P("row", "col", None),
            P("row", "col"), split, split, split, split, P(),
        ),
        out_specs=(split, split, split, P()),
        check_vma=False,
    )
```
